32 devices in a mesh: fsdp: 8 (over y, x, core), seq: 4 (over z).
Axes of the slice: x: 2, y: 2, z: 4, core: 2. Of those that a mesh axis runs over, the one named last changes fastest.
Arguments:
- hidden_in: bfloat16 [8, 1024, 1024], P('fsdp', 'seq'), may hold values from -6 to 6
- cotangent: float32 [8, 1024, 1024], P('fsdp', 'seq'), may hold values from -6 to 6
- doc_ids: int32 [8, 1024], P('fsdp'), may hold values from 0 to 3, never falling along the last dimension, each value on 1 to 512 neighbouring positions
- routes: int32 [8, 1024, 8], P('fsdp', 'seq'), may hold values from 0 to 31, all different within a row; in each aligned block of 256 rows (0 to 255, 256 to 511, ..., all dimensions but the last counted through in order) at most 96 rows name the same one
- gain_attn: bfloat16 [1024], P(('fsdp', 'seq')), may hold values from 0.5 to 1.5
- w_query: bfloat16 [1024, 1024], P(('fsdp', 'seq')), may hold values from -0.1875 to 0.1875
- w_key: bfloat16 [1024, 512], P(('fsdp', 'seq')), may hold values from -0.1875 to 0.1875
- w_value: bfloat16 [1024, 512], P(('fsdp', 'seq')), may hold values from -0.1875 to 0.1875
- w_out: bfloat16 [1024, 1024], P(('fsdp', 'seq')), may hold values from -5 to 5
- gain_ffn: bfloat16 [1024], P(('fsdp', 'seq')), may hold values from 0.5 to 1.5
- w_router: bfloat16 [1024, 32], P(('fsdp', 'seq')), may hold values from -0.1875 to 0.1875
- w_gate: bfloat16 [32, 1024, 512], P('fsdp', 'seq'), may hold values from -0.1875 to 0.1875
- w_up: bfloat16 [32, 1024, 512], P('fsdp', 'seq'), may hold values from -0.1875 to 0.1875
- w_down: bfloat16 [32, 512, 1024], P('fsdp', None, 'seq'), may hold values from -3 to 3
Outputs:
- output: float32 [8, 1024, 1024], P('fsdp', 'seq')
- d_input: float32 [8, 1024, 1024], P('fsdp', 'seq')
- grad_gain_attn: float32 [1024], P(('fsdp', 'seq'))
- grad_query: float32 [1024, 1024], P(('fsdp', 'seq'))
- grad_key: float32 [1024, 512], P(('fsdp', 'seq'))
- grad_value: float32 [1024, 512], P(('fsdp', 'seq'))
- grad_out: float32 [1024, 1024], P(('fsdp', 'seq'))
- grad_gain_ffn: float32 [1024], P(('fsdp', 'seq'))
- grad_router: float32 [1024, 32], P(('fsdp', 'seq'))
- grad_gate: float32 [32, 1024, 512], P('fsdp', 'seq')
- grad_up: float32 [32, 1024, 512], P('fsdp', 'seq')
- grad_down: float32 [32, 512, 1024], P('fsdp', None, 'seq')
The draws below stay inside these ranges and needn't reach their ends.
Inputs may be any that keep to these rules, and one draw needn't show every extreme that they name: `doc_ids`: document numbers never fall along a sequence; a document spans 1 to 512 positions, one exactly 512. `routes`: the 8 experts of a token differ; among the tokens of one device no expert is named more than 96 times, a bound that some block reaches.
All inputs are finite; a program needn't handle non-finite values.
Results may differ from the reference program's by a relative error of at most 0.015.
Values may be sent and summed in bfloat16 or wider, within the bound.
A program may use at most 256 MiB of HBM per device.

```python
import math
import jax
import jax.numpy as jnp
import numpy as np
from jax import lax

D = 1024
HQ = 16
KVH = 8
HD = 64
EXPERTS = 32
TOP = 8
FF_E = 512
LEN = 1024
SEQS = 8
TOKD = 256
CAP = 96
N_SEQ = 4


def shard_levels(own_key, dims, cuts, least, high):
    factor_of = 1.0
    for axis_at, parts in cuts:
        steps = jax.random.uniform(jax.random.fold_in(jax.random.fold_in(own_key, 6), axis_at), (parts,), jnp.float32, least / len(cuts), high / len(cuts))
        factor_of = factor_of * jnp.repeat(jnp.exp(steps), dims[axis_at] // parts).reshape((-1,) + (1,) * (len(dims) - 1 - axis_at))
    return factor_of


def length_profile(number_of, total, most, lean):
    weights = [(1 << 20) // math.isqrt(standing ** lean) + 1 for standing in range(2, number_of + 1)]
    rest, given = total - most - (number_of - 1), [1] * (number_of - 1)
    while rest > 0:
        movable = [i for i in range(number_of - 1) if given[i] < most]
        whole, budget = sum([weights[i] for i in movable]), rest
        for i in movable:
            extra = min(most - given[i], max(1, budget * weights[i] // whole), rest)
            given[i] = given[i] + extra
            rest = rest - extra
    return np.array([most] + given)


def uneven(own_key, amount, total, bound, lean):
    if amount == 2:
        one = jax.random.randint(own_key, (), max(1, total - bound), min(bound, total - 1) + 1)
        return jnp.stack([one, total - one])
    tallies = jnp.asarray(length_profile(amount, total, bound, lean), jnp.int32)
    twos = (amount - 1) // 2
    giver, receiver = tallies[1:1 + 2 * twos:2], tallies[2:2 + 2 * twos:2]
    margin = jnp.minimum(giver - 1, bound - receiver)
    passed = jax.random.randint(jax.random.fold_in(own_key, 1), (twos,), 0, 1 << 20) % (margin + 1)
    tallies = tallies.at[1:1 + 2 * twos:2].set(giver - passed).at[2:2 + 2 * twos:2].set(receiver + passed)
    return tallies[jax.random.permutation(jax.random.fold_in(own_key, 2), amount)]


def assign_block(own_key, own, number, rows, number_of, top, reach, skew):
    order = jax.random.permutation(own_key, number_of)
    heavy_load, ordinary = load_shares(number_of, rows * top, reach, skew, True), load_shares(number_of, rows * top, reach, skew, False)
    places = jnp.arange(number_of)

    def named(lengths, offset_by):
        used = int((lengths > 0).sum())
        fixed = max(1, used // 4)
        shifted = fixed + (places - fixed + offset_by * (used - fixed)) % max(1, number_of - fixed)
        return jnp.zeros((number_of,), jnp.int32).at[order[jnp.where(places < fixed, places, shifted)]].set(jnp.asarray(lengths, jnp.int32))

    lengths = jnp.where(number % 4 == 0, named(heavy_load, number // 4), named(ordinary, number - number // 4 - 1))
    mixed = jax.random.permutation(jax.random.fold_in(own, 3), number_of)
    giver, taker = mixed[0:number_of // 2 * 2:2], mixed[1:number_of // 2 * 2:2]
    slack = jnp.minimum(lengths[giver] - 1, reach - lengths[taker]) // 2
    slack = jnp.where((giver == order[0]) | (taker == order[0]) | (lengths[taker] == 0), 0, jnp.maximum(slack, 0))
    shifted = jax.random.randint(jax.random.fold_in(own, 4), (number_of // 2,), 0, 1 << 20) % (slack + 1)
    lengths = lengths.at[giver].add(-shifted).at[taker].add(shifted)
    members = jnp.searchsorted(jnp.cumsum(lengths), jnp.arange(rows * top), side="right").astype(jnp.int32)
    grid = members.reshape(top, rows).T
    grid = grid[jax.random.permutation(jax.random.fold_in(own, 1), rows)]
    offset_by = jax.random.randint(jax.random.fold_in(own, 2), (rows, 1), 0, top)
    return jnp.take_along_axis(grid, (jnp.arange(top)[None, :] + offset_by) % top, axis=1)


def load_shares(amount, total, limit, skew, full):
    loads = [(1 << 20) // math.isqrt(standing ** skew) + 1 for standing in range(1, amount + 1)]
    largest = limit if full else min(limit, max(-(-total // amount), total * loads[0] // sum(loads)))
    least = 1 if total - largest >= amount - 1 else 0
    counts, surplus = [largest] + [least] * (amount - 1), total - largest - least * (amount - 1)
    while surplus > 0:
        free = [i for i in range(1, amount) if counts[i] < largest] or [i for i in range(1, amount) if counts[i] < limit]
        mass, budget = sum([loads[i] for i in free]), surplus
        for i in free:
            addition = min(limit - counts[i], max(1, budget * loads[i] // mass), surplus)
            counts[i] = counts[i] + addition
            surplus = surplus - addition
    return np.array(counts)


def bell_draw(stream_key, dims, spread, bound, shards=(), kind=jnp.bfloat16):
    result = jax.random.normal(stream_key, dims, jnp.float32) * spread
    if len(shards) > 0:
        result = shard_levels(stream_key, dims, shards, -0.22, 0.18) * result
    return jnp.clip(result, min=-bound, max=bound).astype(kind)


def setup_inputs(seed: int = 0) -> dict:
    key_list = jax.random.split(jax.random.key(seed), 15)
    hidden_in = bell_draw(key_list[0], (SEQS, LEN, D), 1.0, 6.0, ((0, 8), (1, 4)))
    cotangent = bell_draw(key_list[1], (SEQS, LEN, D), 1.0, 6.0, ((0, 8), (1, 4)), jnp.float32)
    doc_ids = jax.vmap(lambda own: jnp.searchsorted(jnp.cumsum(uneven(own, 4, LEN, LEN // 2, 1)), jnp.arange(LEN), side="right"))(jax.random.split(key_list[2], SEQS)).reshape((SEQS, LEN)).astype(jnp.int32)
    routes_keys = jax.random.split(jax.random.fold_in(key_list[3], 1), SEQS * LEN // TOKD)
    routes_turns = jax.random.permutation(jax.random.fold_in(key_list[3], 3), SEQS * LEN // TOKD)
    routes = jax.vmap(lambda own, number: assign_block(jax.random.fold_in(key_list[3], 2), own, number, TOKD, EXPERTS, TOP, CAP, 2))(routes_keys, routes_turns).reshape((SEQS, LEN, TOP))
    gain_attn = jnp.clip(1.0 + 0.1 * jax.random.normal(key_list[4], (D,), jnp.float32), 0.5, 1.5).astype(jnp.bfloat16)
    w_query = bell_draw(key_list[5], (D, HQ * HD), D ** -0.5, 0.1875, ((0, 32),))
    w_key = bell_draw(key_list[6], (D, KVH * HD), D ** -0.5, 0.1875, ((0, 32),))
    w_value = bell_draw(key_list[7], (D, KVH * HD), D ** -0.5, 0.1875, ((0, 32),))
    w_out = bell_draw(key_list[8], (HQ * HD, D), 1.0, 5.0, ((0, 32),))
    gain_ffn = jnp.clip(1.0 + 0.1 * jax.random.normal(key_list[9], (D,), jnp.float32), 0.5, 1.5).astype(jnp.bfloat16)
    w_router = bell_draw(key_list[10], (D, EXPERTS), D ** -0.5, 0.1875, ((0, 32),))
    w_gate = bell_draw(key_list[11], (EXPERTS, D, FF_E), D ** -0.5, 0.1875, ((0, 8), (1, 4)))
    w_up = bell_draw(key_list[12], (EXPERTS, D, FF_E), D ** -0.5, 0.1875, ((0, 8), (1, 4)))
    w_down = bell_draw(key_list[13], (EXPERTS, FF_E, D), 0.5, 3.0, ((0, 8), (2, 4)))
    return dict(hidden_in=hidden_in, cotangent=cotangent, doc_ids=doc_ids, routes=routes, gain_attn=gain_attn, w_query=w_query, w_key=w_key, w_value=w_value, w_out=w_out, gain_ffn=gain_ffn, w_router=w_router, w_gate=w_gate, w_up=w_up, w_down=w_down)


EPS = 1e-06
ATTN_MULT = 0.015625
RESID_MULT = 0.22
THETA = 10000.0
NEG_FILL = -1e+30

def rounded(values):
    return lax.optimization_barrier(values.astype(jnp.bfloat16))

def rope_tables(positions, head_dim):
    half_dim = head_dim // 2
    frequency = THETA ** (-(jnp.arange(half_dim, dtype=jnp.float32) * 2.0 / head_dim))
    phases = positions.astype(jnp.float32)[:, None] * frequency[None, :]
    return (jnp.cos(phases), jnp.sin(phases))

def rotate(values, cosine, sine_tab):
    half_dim = values.shape[-1] // 2
    first_half = values[..., :half_dim]
    second_half = values[..., half_dim:]
    cos_b = cosine[:, None, :]
    sin_b = sine_tab[:, None, :]
    return jnp.concatenate([first_half * cos_b - second_half * sin_b, second_half * cos_b + first_half * sin_b], axis=-1)

def unrotate(grad_vals, cosine, sine_tab):
    half_dim = grad_vals.shape[-1] // 2
    first_half = grad_vals[..., :half_dim]
    second_half = grad_vals[..., half_dim:]
    cos_b = cosine[:, None, :]
    sin_b = sine_tab[:, None, :]
    return jnp.concatenate([first_half * cos_b + second_half * sin_b, second_half * cos_b - first_half * sin_b], axis=-1)

def rms_scale(values):
    return lax.rsqrt(lax.optimization_barrier(jnp.mean(values * values, axis=-1, keepdims=True)) + EPS)

def norm_backward(inputs, scale, gain, d_normed):
    upstream = gain * d_normed
    d_inputs = scale * upstream - inputs * scale ** 3 * lax.optimization_barrier(jnp.mean(upstream * inputs, axis=-1, keepdims=True))
    d_gain = lax.optimization_barrier(jnp.sum(d_normed * inputs * scale, axis=0))
    return (d_inputs, d_gain)

def head_scores(query, keys, allowed):
    scores = jnp.einsum('qgd,sd->gqs', query.astype(jnp.float32), keys.astype(jnp.float32)) * ATTN_MULT
    return jnp.where(allowed[None], scores, NEG_FILL)

def attend_forward(query, keys, values, allowed):
    scores = head_scores(query, keys, allowed)
    top_val = lax.optimization_barrier(jnp.max(scores, axis=-1, keepdims=True))
    expo_vals = jnp.exp(scores - top_val)
    row_total = lax.optimization_barrier(jnp.sum(expo_vals, axis=-1, keepdims=True))
    log_total = top_val[..., 0] + jnp.log(row_total[..., 0])
    prob_vals = rounded(expo_vals / row_total)
    attended = jnp.einsum('gqs,sd->qgd', prob_vals.astype(jnp.float32), values.astype(jnp.float32))
    return (rounded(attended), log_total)

def attend_backward(query, keys, values, attended, log_total, d_attended, allowed):
    scores = head_scores(query, keys, allowed)
    prob_vals = jnp.exp(scores - log_total[..., None])
    prob_low = rounded(prob_vals)
    d_values = jnp.einsum('gqs,qgd->sd', prob_low.astype(jnp.float32), d_attended.astype(jnp.float32))
    d_prob = jnp.einsum('qgd,sd->gqs', d_attended.astype(jnp.float32), values.astype(jnp.float32))
    row_delta = jnp.transpose(lax.optimization_barrier(jnp.sum(d_attended.astype(jnp.float32) * attended.astype(jnp.float32), axis=-1)), (1, 0))
    d_score = rounded(prob_vals * (d_prob - row_delta[..., None]) * ATTN_MULT)
    d_query = jnp.einsum('gqs,sd->qgd', d_score.astype(jnp.float32), keys.astype(jnp.float32))
    d_keys = jnp.einsum('gqs,qgd->sd', d_score.astype(jnp.float32), query.astype(jnp.float32))
    return (d_query, d_keys, d_values)

def reference(hidden_in, cotangent, doc_ids, routes, gain_attn, w_query, w_key, w_value, w_out, gain_ffn, w_router, w_gate, w_up, w_down):
    group_size = HQ // KVH
    seq_cap = N_SEQ * CAP
    n_slots = EXPERTS * seq_cap
    positions = jnp.arange(LEN, dtype=jnp.int32)
    cosine, sine_tab = rope_tables(positions, HD)
    causal = positions[:, None] >= positions[None, :]
    gain_one = gain_attn.astype(jnp.float32)
    gain_two = gain_ffn.astype(jnp.float32)
    gate_wide = w_gate.astype(jnp.float32)
    up_wide = w_up.astype(jnp.float32)
    down_wide = w_down.astype(jnp.float32)
    expert_ids = jnp.arange(EXPERTS, dtype=jnp.int32)

    def one_sequence(carry, inputs):
        tok_in, grad_in, seg_row, route_row = inputs
        tokens = tok_in.astype(jnp.float32)
        scale_one = rms_scale(tokens)
        normed_one = rounded(tokens * scale_one * gain_one)
        query = jnp.dot(normed_one, w_query, preferred_element_type=jnp.float32).reshape(LEN, HQ, HD)
        keys = jnp.dot(normed_one, w_key, preferred_element_type=jnp.float32).reshape(LEN, KVH, HD)
        query = rounded(rotate(query, cosine, sine_tab)).reshape(LEN, KVH, group_size, HD)
        keys = rounded(rotate(keys, cosine, sine_tab))
        values = rounded(jnp.dot(normed_one, w_value, preferred_element_type=jnp.float32)).reshape(LEN, KVH, HD)
        allowed = causal & (seg_row[:, None] == seg_row[None, :])
        q_by_kv = jnp.transpose(query, (1, 0, 2, 3))
        k_by_kv = jnp.transpose(keys, (1, 0, 2))
        v_by_kv = jnp.transpose(values, (1, 0, 2))

        def forward_head(operands):
            return attend_forward(operands[0], operands[1], operands[2], allowed)
        attended, log_total = lax.map(forward_head, (q_by_kv, k_by_kv, v_by_kv))
        attn_flat = jnp.transpose(attended, (1, 0, 2, 3)).reshape(LEN, HQ * HD)
        branch = jnp.dot(attn_flat, w_out, preferred_element_type=jnp.float32)
        resid = tokens + RESID_MULT * branch
        scale_two = rms_scale(resid)
        normed_two = rounded(resid * scale_two * gain_two)
        logits = jnp.dot(normed_two, w_router, preferred_element_type=jnp.float32)
        chosen = jnp.take_along_axis(logits, route_row, axis=1)
        top_val = lax.optimization_barrier(jnp.max(chosen, axis=-1, keepdims=True))
        expo_vals = jnp.exp(chosen - top_val)
        gates = expo_vals / lax.optimization_barrier(jnp.sum(expo_vals, axis=-1, keepdims=True))
        flat_route = route_row.reshape(-1)
        hits = (flat_route[:, None] == expert_ids[None, :]).astype(jnp.int32)
        before = jnp.cumsum(hits, axis=0, dtype=jnp.int32) - hits
        place = lax.optimization_barrier(jnp.sum(before * hits, axis=1, dtype=jnp.int32))
        slot_of = (flat_route * seq_cap + place).astype(jnp.int32)
        token_of = (jnp.arange(LEN * TOP, dtype=jnp.int32) // TOP).astype(jnp.int32)
        slot_token = jnp.zeros((n_slots,), jnp.int32).at[slot_of].set(token_of)
        slot_live = jnp.zeros((n_slots,), jnp.bfloat16).at[slot_of].set(jnp.ones((LEN * TOP,), jnp.bfloat16))
        dispatched = (jnp.take(normed_two, slot_token, axis=0) * slot_live[:, None]).reshape(EXPERTS, seq_cap, D)
        slot_in = dispatched.astype(jnp.float32)
        pre_gate = jnp.einsum('ecd,edf->ecf', slot_in, gate_wide)
        pre_up = jnp.einsum('ecd,edf->ecf', slot_in, up_wide)
        sigm = jax.nn.sigmoid(pre_gate)
        act = rounded(pre_gate * sigm * pre_up)
        expert_out = rounded(jnp.einsum('ecf,efd->ecd', act.astype(jnp.float32), down_wide)).reshape(n_slots, D)
        picked = jnp.take(expert_out, slot_of, axis=0).reshape(LEN, TOP, D).astype(jnp.float32)
        moe = lax.optimization_barrier(jnp.sum(gates[:, :, None] * picked, axis=1))
        output = resid + RESID_MULT * moe
        d_moe = RESID_MULT * grad_in
        d_gates = lax.optimization_barrier(jnp.sum(d_moe[:, None, :] * picked, axis=-1))
        d_assign = rounded(gates[:, :, None] * d_moe[:, None, :]).reshape(LEN * TOP, D)
        d_slots = jnp.zeros((n_slots, D), jnp.bfloat16).at[slot_of].set(d_assign).reshape(EXPERTS, seq_cap, D)
        d_slots_wide = d_slots.astype(jnp.float32)
        d_act = jnp.einsum('ecd,efd->ecf', d_slots_wide, down_wide)
        grad_down_part = jnp.einsum('ecf,ecd->efd', act.astype(jnp.float32), d_slots_wide)
        d_up = rounded(d_act * pre_gate * sigm)
        d_pre_gate = rounded(d_act * pre_up * sigm * (1.0 + pre_gate * (1.0 - sigm)))
        grad_gate_part = jnp.einsum('ecd,ecf->edf', slot_in, d_pre_gate.astype(jnp.float32))
        grad_up_part = jnp.einsum('ecd,ecf->edf', slot_in, d_up.astype(jnp.float32))
        d_expert_in = rounded(jnp.einsum('ecf,edf->ecd', d_pre_gate.astype(jnp.float32), gate_wide) + jnp.einsum('ecf,edf->ecd', d_up.astype(jnp.float32), up_wide)).reshape(n_slots, D)
        d_from_experts = lax.optimization_barrier(jnp.sum(jnp.take(d_expert_in, slot_of, axis=0).reshape(LEN, TOP, D).astype(jnp.float32), axis=1))
        d_chosen = gates * (d_gates - lax.optimization_barrier(jnp.sum(gates * d_gates, axis=-1, keepdims=True)))
        onehot = (route_row[:, :, None] == expert_ids[None, None, :]).astype(jnp.float32)
        d_logits = rounded(lax.optimization_barrier(jnp.sum(d_chosen[:, :, None] * onehot, axis=1)))
        d_normed_two = d_from_experts + jnp.dot(d_logits, w_router.T, preferred_element_type=jnp.float32)
        grad_router_part = jnp.dot(normed_two.T, d_logits, preferred_element_type=jnp.float32)
        d_norm_two, grad_gain_two = norm_backward(resid, scale_two, gain_two, d_normed_two)
        d_resid = grad_in + d_norm_two
        d_branch = rounded(RESID_MULT * d_resid)
        grad_out_part = jnp.dot(attn_flat.T, d_branch, preferred_element_type=jnp.float32)
        d_attn = rounded(jnp.dot(d_branch, w_out.T, preferred_element_type=jnp.float32))
        d_attn_by_kv = jnp.transpose(d_attn.reshape(LEN, KVH, group_size, HD), (1, 0, 2, 3))

        def backward_head(operands):
            return attend_backward(operands[0], operands[1], operands[2], operands[3], operands[4], operands[5], allowed)
        d_query, d_keys, d_values = lax.map(backward_head, (q_by_kv, k_by_kv, v_by_kv, attended, log_total, d_attn_by_kv))
        d_query = jnp.transpose(d_query, (1, 0, 2, 3)).reshape(LEN, HQ, HD)
        d_query = rounded(unrotate(d_query, cosine, sine_tab)).reshape(LEN, HQ * HD)
        d_keys = rounded(unrotate(jnp.transpose(d_keys, (1, 0, 2)), cosine, sine_tab)).reshape(LEN, KVH * HD)
        d_values = rounded(jnp.transpose(d_values, (1, 0, 2))).reshape(LEN, KVH * HD)
        d_normed_one = jnp.dot(d_query, w_query.T, preferred_element_type=jnp.float32) + jnp.dot(d_keys, w_key.T, preferred_element_type=jnp.float32) + jnp.dot(d_values, w_value.T, preferred_element_type=jnp.float32)
        grad_query_part = jnp.dot(normed_one.T, d_query, preferred_element_type=jnp.float32)
        grad_key_part = jnp.dot(normed_one.T, d_keys, preferred_element_type=jnp.float32)
        grad_value_part = jnp.dot(normed_one.T, d_values, preferred_element_type=jnp.float32)
        d_norm_one, grad_gain_one = norm_backward(tokens, scale_one, gain_one, d_normed_one)
        d_input = d_resid + d_norm_one
        new_carry = (carry[0] + grad_gain_one, carry[1] + grad_query_part, carry[2] + grad_key_part, carry[3] + grad_value_part, carry[4] + grad_out_part, carry[5] + grad_gain_two, carry[6] + grad_router_part, carry[7] + grad_gate_part, carry[8] + grad_up_part, carry[9] + grad_down_part)
        return (new_carry, (output, d_input))
    init = (jnp.zeros((D,), jnp.float32), jnp.zeros((D, HQ * HD), jnp.float32), jnp.zeros((D, KVH * HD), jnp.float32), jnp.zeros((D, KVH * HD), jnp.float32), jnp.zeros((HQ * HD, D), jnp.float32), jnp.zeros((D,), jnp.float32), jnp.zeros((D, EXPERTS), jnp.float32), jnp.zeros((EXPERTS, D, FF_E), jnp.float32), jnp.zeros((EXPERTS, D, FF_E), jnp.float32), jnp.zeros((EXPERTS, FF_E, D), jnp.float32))
    totals, stacked = lax.scan(one_sequence, init, (hidden_in, cotangent, doc_ids, routes))
    return (stacked[0], stacked[1], totals[0], totals[1], totals[2], totals[3], totals[4], totals[5], totals[6], totals[7], totals[8], totals[9])
```

```python
import jax
import jax.numpy as jnp
from jax import lax
from jax.sharding import PartitionSpec as P

HD = 64


EPS = 1e-06
ATTN_MULT = 0.015625
RESID_MULT = 0.22
THETA = 10000.0
NEG_FILL = -1e30


def rope_tables(positions, head_dim):
    half_dim = head_dim // 2
    frequency = THETA ** (-(jnp.arange(half_dim, dtype=jnp.float32) * 2.0 / head_dim))
    phases = positions.astype(jnp.float32)[:, None] * frequency[None, :]
    return (jnp.cos(phases), jnp.sin(phases))


def rotate(values, cosine, sine_tab):
    half_dim = values.shape[-1] // 2
    first_half = values[..., :half_dim]
    second_half = values[..., half_dim:]
    cos_b = cosine[:, None, :]
    sin_b = sine_tab[:, None, :]
    return jnp.concatenate(
        [first_half * cos_b - second_half * sin_b, second_half * cos_b + first_half * sin_b],
        axis=-1,
    )


def unrotate(grad_vals, cosine, sine_tab):
    half_dim = grad_vals.shape[-1] // 2
    first_half = grad_vals[..., :half_dim]
    second_half = grad_vals[..., half_dim:]
    cos_b = cosine[:, None, :]
    sin_b = sine_tab[:, None, :]
    return jnp.concatenate(
        [first_half * cos_b + second_half * sin_b, second_half * cos_b - first_half * sin_b],
        axis=-1,
    )


def rms_scale(values):
    return lax.rsqrt(jnp.mean(values * values, axis=-1, keepdims=True) + EPS)


def norm_backward(inputs, scale, gain, d_normed):
    upstream = gain * d_normed
    d_inputs = scale * upstream - inputs * scale**3 * jnp.mean(
        upstream * inputs, axis=-1, keepdims=True
    )
    d_gain = jnp.sum(d_normed * inputs * scale, axis=0)
    return (d_inputs, d_gain)


def on_device(
    hidden_in,
    cotangent,
    doc_ids,
    routes,
    gain_attn,
    w_query,
    w_key,
    w_value,
    w_out,
    gain_ffn,
    w_router,
    w_gate,
    w_up,
    w_down,
):
    n_seq = lax.axis_size("seq")
    n_fsdp = lax.axis_size("fsdp")
    tok_rows = hidden_in.shape[1]
    width = hidden_in.shape[2]
    seq_len = tok_rows * n_seq
    top_k = routes.shape[2]
    n_expert = w_router.shape[1]
    local_exp = w_gate.shape[0]
    head_dim = HD
    q_width = w_query.shape[1]
    kv_width = w_key.shape[1]
    heads_here = q_width // head_dim // n_seq
    kv_here = kv_width // head_dim // n_seq
    group_size = heads_here // kv_here
    slot_cap = 3 * tok_rows * top_k // (2 * n_expert)
    f32, bf16 = jnp.float32, jnp.bfloat16
    row_own = w_query.shape[0]
    model = row_own * n_fsdp * n_seq

    def column(gain):
        return jnp.pad(gain[:, None], ((0, 0), (0, 127)))

    packed = jnp.concatenate(
        [
            w_query,
            w_key,
            w_value,
            column(gain_attn),
            w_out,
            jnp.pad(w_router, ((0, 0), (0, 128 - n_expert % 128))),
            column(gain_ffn),
        ],
        axis=1,
    )
    full = lax.all_gather(packed, ("fsdp", "seq"), axis=0, tiled=True)
    qkv_width = q_width + 2 * kv_width
    out_at = qkv_width + 128
    router_at = out_at + w_out.shape[1]
    gain_at = packed.shape[1] - 128
    full_qkv = full[:, :qkv_width]
    gain_one = full[:, qkv_width].astype(f32)
    full_out = full[:, out_at:router_at]
    full_router = full[:, router_at : router_at + n_expert]
    gain_two = full[:, gain_at].astype(f32)
    gathered_gate, gathered_up, gathered_down = (
        lax.all_gather(w_gate, "seq", axis=1, tiled=True),
        lax.all_gather(w_up, "seq", axis=1, tiled=True),
        lax.all_gather(w_down, "seq", axis=2, tiled=True),
    )

    def to_all(block):
        return lax.all_to_all(
            jnp.broadcast_to(block[None], (n_fsdp,) + block.shape),
            "fsdp",
            split_axis=0,
            concat_axis=0,
            tiled=True,
        )

    grad_in = cotangent[0]
    d_moe_all = to_all((RESID_MULT * grad_in).astype(bf16))
    routes_all = to_all(routes[0].T)
    tokens = hidden_in[0].astype(f32)
    scale_one = rms_scale(tokens)
    normed_one = (tokens * scale_one * gain_one).astype(bf16)
    tok_pos = lax.axis_index("seq") * tok_rows + jnp.arange(tok_rows, dtype=jnp.int32)
    cos_tok, sin_tok = rope_tables(tok_pos, head_dim)
    qkv = jnp.dot(normed_one, full_qkv, preferred_element_type=f32)
    query = qkv[:, :q_width].reshape(tok_rows, -1, head_dim)
    keys_tok = qkv[:, q_width : q_width + kv_width].reshape(tok_rows, -1, head_dim)
    query = (
        rotate(query, cos_tok, sin_tok).astype(bf16).reshape(tok_rows, n_seq, heads_here * head_dim)
    )
    keys_tok = (
        rotate(keys_tok, cos_tok, sin_tok).astype(bf16).reshape(tok_rows, n_seq, kv_here * head_dim)
    )
    values_tok = qkv[:, q_width + kv_width :].astype(bf16)
    key_value = jnp.concatenate(
        [query, keys_tok, values_tok.reshape(tok_rows, n_seq, kv_here * head_dim)], axis=-1
    )
    recv = lax.all_to_all(key_value, "seq", split_axis=1, concat_axis=0, tiled=True)[:, 0]
    q_here = heads_here * head_dim
    k_end = q_here + kv_here * head_dim
    q_heads = recv[:, :q_here].reshape(seq_len, kv_here, group_size, head_dim)
    k_heads = recv[:, q_here:k_end].reshape(seq_len, kv_here, head_dim)
    v_heads = recv[:, k_end:].reshape(seq_len, kv_here, head_dim)
    doc_row = doc_ids[0]
    key_pos = jnp.arange(seq_len, dtype=jnp.int32)
    block_rows = min(512, seq_len)
    starts = list(range(0, seq_len, block_rows))

    def block_scores(row_start):
        row_end = row_start + block_rows
        q_blk = q_heads[row_start:row_end]
        query_pos = row_start + jnp.arange(block_rows, dtype=jnp.int32)
        allowed = (query_pos[:, None] >= key_pos[None, :row_end]) & (
            doc_row[row_start:row_end][:, None] == doc_row[None, :row_end]
        )
        scores = (
            jnp.einsum("qkgd,skd->kgqs", q_blk, k_heads[:row_end], preferred_element_type=f32)
            * ATTN_MULT
        )
        return (q_blk, jnp.where(allowed[None, None], scores, NEG_FILL))

    attn_parts = []
    lse_parts = []
    for row_start in starts:
        q_blk, scores = block_scores(row_start)
        top_val = jnp.max(scores, axis=-1, keepdims=True)
        expo_vals = jnp.exp(scores - top_val)
        row_total = jnp.sum(expo_vals, axis=-1, keepdims=True)
        lse_parts.append(top_val[..., 0] + jnp.log(row_total[..., 0]))
        prob_vals = (expo_vals / row_total).astype(bf16)
        attn_parts.append(
            jnp.einsum(
                "kgqs,skd->qkgd",
                prob_vals,
                v_heads[: row_start + block_rows],
                preferred_element_type=f32,
            ).astype(bf16)
        )
    attn_heads = jnp.concatenate(attn_parts, axis=0)
    attn_tok = lax.all_to_all(
        attn_heads.reshape(seq_len, 1, q_here),
        "seq",
        split_axis=0,
        concat_axis=1,
        tiled=True,
    ).reshape(tok_rows, q_width)
    branch = jnp.dot(attn_tok, full_out, preferred_element_type=f32)
    resid = tokens + RESID_MULT * branch
    scale_two = rms_scale(resid)
    normed_two = (resid * scale_two * gain_two).astype(bf16)
    tok_all = to_all(normed_two)

    def dense_gates(logits, route_kt):
        experts = jnp.arange(n_expert, dtype=jnp.int32)
        picked = jnp.any(route_kt[..., None] == experts, axis=-3)
        top_val = jnp.max(jnp.where(picked, logits, NEG_FILL), axis=-1, keepdims=True)
        expo_vals = jnp.where(picked, jnp.exp(jnp.where(picked, logits - top_val, 0.0)), 0.0)
        return picked, expo_vals / jnp.sum(expo_vals, axis=-1, keepdims=True)

    logits_own = jnp.dot(normed_two, full_router, preferred_element_type=f32)
    _, gates = dense_gates(logits_own, routes[0].T)
    first = lax.axis_index("fsdp") * local_exp
    picked_all, gates_all = dense_gates(
        jnp.einsum("std,de->ste", tok_all, full_router, preferred_element_type=f32), routes_all
    )
    own_picked = jnp.transpose(
        lax.dynamic_slice_in_dim(picked_all, first, local_exp, axis=2), (0, 2, 1)
    )
    own_gates = jnp.transpose(
        lax.dynamic_slice_in_dim(gates_all, first, local_exp, axis=2), (0, 2, 1)
    )
    earlier = (
        jnp.arange(tok_rows, dtype=jnp.int32)[:, None]
        < jnp.arange(tok_rows, dtype=jnp.int32)[None, :]
    ).astype(bf16)
    place = jnp.einsum(
        "seu,ut->set", own_picked.astype(bf16), earlier, preferred_element_type=f32
    ).astype(jnp.int32)
    place = jnp.where(own_picked, place, -1)
    slot_hit = place[:, :, None, :] == jnp.arange(slot_cap, dtype=jnp.int32)[:, None]
    slot_map = slot_hit.astype(bf16)
    slot_gate = jnp.sum(jnp.where(slot_hit, own_gates[:, :, None, :], 0.0), axis=-1)
    slot_gate = jnp.transpose(slot_gate, (1, 0, 2)).reshape(local_exp, n_fsdp * slot_cap, 1)
    slot_flat = slot_map.reshape(n_fsdp, local_exp * slot_cap, tok_rows)

    def to_slots(rows):
        found = jnp.einsum("sjt,std->sjd", slot_flat, rows, preferred_element_type=f32)
        found = found.astype(bf16).reshape(n_fsdp, local_exp, slot_cap, width)
        return jnp.transpose(found, (1, 0, 2, 3)).reshape(local_exp, n_fsdp * slot_cap, width)

    def from_slots(rows):
        rows = rows.reshape(local_exp, n_fsdp, slot_cap, width)
        rows = jnp.transpose(rows, (1, 0, 2, 3)).reshape(n_fsdp, local_exp * slot_cap, width)
        part = jnp.einsum("sjt,sjd->std", slot_flat, rows, preferred_element_type=f32)
        part = lax.all_to_all(part.astype(bf16), "fsdp", split_axis=0, concat_axis=0, tiled=True)
        return jnp.sum(part.astype(f32), axis=0)

    d_rows = to_slots(d_moe_all)
    inbound = to_slots(tok_all)
    pre_gate = jnp.einsum("ead,edf->eaf", inbound, gathered_gate, preferred_element_type=f32)
    pre_up = jnp.einsum("ead,edf->eaf", inbound, gathered_up, preferred_element_type=f32)
    sigm = jax.nn.sigmoid(pre_gate)
    act = pre_gate * sigm * pre_up
    act_gated = (act * slot_gate).astype(bf16)
    d_plain = jnp.einsum("ead,efd->eaf", d_rows, gathered_down, preferred_element_type=f32)
    slot_d_gate = jnp.sum(act * d_plain, axis=-1)
    d_act = d_plain * slot_gate
    d_up = (d_act * pre_gate * sigm).astype(bf16)
    d_pre_gate = (d_act * pre_up * sigm * (1.0 + pre_gate * (1.0 - sigm))).astype(bf16)
    slot_d_gate = jnp.transpose(
        slot_d_gate.reshape(local_exp, n_fsdp, slot_cap), (1, 0, 2)
    )
    d_gates_part = jnp.sum(jnp.where(slot_hit, slot_d_gate[..., None], 0.0), axis=2)
    d_gates = lax.all_to_all(d_gates_part, "fsdp", split_axis=0, concat_axis=0, tiled=True)
    d_gates = d_gates.reshape(n_expert, tok_rows).T
    d_inputs = (
        jnp.einsum("eaf,edf->ead", d_pre_gate, gathered_gate, preferred_element_type=f32)
        + jnp.einsum("eaf,edf->ead", d_up, gathered_up, preferred_element_type=f32)
    ).astype(bf16)
    d_from_experts = from_slots(d_inputs)
    expert_out = jnp.einsum("eaf,efd->ead", act_gated, gathered_down, preferred_element_type=f32)
    output = resid + RESID_MULT * from_slots(expert_out.astype(bf16))
    grad_gate = jnp.einsum("ead,eaf->edf", inbound, d_pre_gate, preferred_element_type=f32)
    grad_up = jnp.einsum("ead,eaf->edf", inbound, d_up, preferred_element_type=f32)
    grad_down = jnp.einsum("ead,eaf->efd", d_rows, act_gated, preferred_element_type=f32)

    def sum_seq(grad, axis):
        shape = grad.shape[:axis] + (n_seq, grad.shape[axis] // n_seq) + grad.shape[axis + 1 :]
        parts = jnp.moveaxis(grad.astype(bf16).reshape(shape), axis, 0)
        parts = lax.all_to_all(parts, "seq", split_axis=0, concat_axis=0, tiled=True)
        return jnp.sum(parts.astype(f32), axis=0)

    owned_gate, owned_up, owned_down = (
        sum_seq(grad_gate, 1),
        sum_seq(grad_up, 1),
        sum_seq(grad_down, 2),
    )

    def sum_all(grad):
        parts = lax.all_to_all(
            grad.astype(bf16).reshape(n_fsdp, model // n_fsdp, -1),
            "fsdp",
            split_axis=0,
            concat_axis=0,
            tiled=True,
        )
        part = jnp.sum(parts.astype(f32), axis=0).astype(bf16)
        parts = lax.all_to_all(
            part.reshape(n_seq, row_own, -1), "seq", split_axis=0, concat_axis=0, tiled=True
        )
        return jnp.sum(parts.astype(f32), axis=0)

    d_chosen = gates * (d_gates - jnp.sum(gates * d_gates, axis=-1, keepdims=True))
    d_logits = d_chosen.astype(bf16)
    d_normed_two = d_from_experts + jnp.einsum(
        "te,de->td", d_logits, full_router, preferred_element_type=f32
    )
    grad_router = jnp.einsum("td,te->de", normed_two, d_logits, preferred_element_type=f32)
    d_norm_two, grad_gain_two = norm_backward(resid, scale_two, gain_two, d_normed_two)
    d_resid = grad_in + d_norm_two
    d_branch = (RESID_MULT * d_resid).astype(bf16)
    grad_out = jnp.einsum("tq,td->qd", attn_tok, d_branch, preferred_element_type=f32)
    d_attn = jnp.einsum("td,qd->tq", d_branch, full_out, preferred_element_type=f32).astype(bf16)
    own_early = sum_all(
        jnp.concatenate(
            [grad_out, jnp.pad(grad_router, ((0, 0), (0, 127 - n_expert))), grad_gain_two[:, None]],
            axis=1,
        )
    )
    d_heads = lax.all_to_all(
        d_attn.reshape(tok_rows, n_seq, q_here),
        "seq",
        split_axis=1,
        concat_axis=0,
        tiled=True,
    ).reshape(seq_len, kv_here, group_size, head_dim)
    d_query_parts = []
    d_key_sum = jnp.zeros((seq_len, kv_here, head_dim), f32)
    d_val_sum = jnp.zeros((seq_len, kv_here, head_dim), f32)
    for step, row_start in enumerate(starts):
        row_end = row_start + block_rows
        q_blk, scores = block_scores(row_start)
        prob_vals = jnp.exp(scores - lse_parts[step][..., None])
        d_out_blk = d_heads[row_start:row_end]
        attn_blk = attn_heads[row_start:row_end]
        d_val_sum = d_val_sum.at[:row_end].add(
            jnp.einsum(
                "kgqs,qkgd->skd", prob_vals.astype(bf16), d_out_blk, preferred_element_type=f32
            )
        )
        d_prob = jnp.einsum(
            "qkgd,skd->kgqs", d_out_blk, v_heads[:row_end], preferred_element_type=f32
        )
        row_delta = jnp.transpose(
            jnp.sum(d_out_blk.astype(f32) * attn_blk.astype(f32), axis=-1), (1, 2, 0)
        )
        d_score = (prob_vals * (d_prob - row_delta[..., None]) * ATTN_MULT).astype(bf16)
        d_query_parts.append(
            jnp.einsum("kgqs,skd->qkgd", d_score, k_heads[:row_end], preferred_element_type=f32)
        )
        d_key_sum = d_key_sum.at[:row_end].add(
            jnp.einsum("kgqs,qkgd->skd", d_score, q_blk, preferred_element_type=f32)
        )
    cos_full, sin_full = rope_tables(key_pos, head_dim)
    d_query_all = jnp.concatenate(d_query_parts, axis=0).reshape(seq_len, heads_here, head_dim)
    d_query_rot = unrotate(d_query_all, cos_full, sin_full).astype(bf16).reshape(seq_len, 1, q_here)
    d_key_rot = (
        unrotate(d_key_sum, cos_full, sin_full).astype(bf16).reshape(seq_len, 1, kv_here * head_dim)
    )
    d_val_low = d_val_sum.astype(bf16).reshape(seq_len, 1, kv_here * head_dim)
    d_recv = lax.all_to_all(
        jnp.concatenate([d_query_rot, d_key_rot, d_val_low], axis=-1),
        "seq",
        split_axis=0,
        concat_axis=1,
        tiled=True,
    )
    d_qkv = jnp.concatenate(
        [
            d_recv[:, :, :q_here].reshape(tok_rows, q_width),
            d_recv[:, :, q_here:k_end].reshape(tok_rows, kv_width),
            d_recv[:, :, k_end:].reshape(tok_rows, kv_width),
        ],
        axis=1,
    )
    d_normed_one = jnp.einsum("tq,dq->td", d_qkv, full_qkv, preferred_element_type=f32)
    grad_qkv = jnp.einsum("td,tq->dq", normed_one, d_qkv, preferred_element_type=f32)
    d_norm_one, grad_gain_one = norm_backward(tokens, scale_one, gain_one, d_normed_one)
    d_input = d_resid + d_norm_one
    own_late = sum_all(
        jnp.concatenate([grad_qkv, jnp.pad(grad_gain_one[:, None], ((0, 0), (0, 127)))], axis=1)
    )
    return (
        output[None],
        d_input[None],
        own_late[:, qkv_width],
        own_late[:, :q_width],
        own_late[:, q_width : q_width + kv_width],
        own_late[:, q_width + kv_width : qkv_width],
        own_early[:, :width],
        own_early[:, width + 127],
        own_early[:, width : width + n_expert],
        owned_gate,
        owned_up,
        owned_down,
    )


def solution(mesh):
    placed = (
        P("fsdp", "seq", None),
        P("fsdp", "seq", None),
        P("fsdp", None),
        P("fsdp", "seq", None),
        P(("fsdp", "seq")),
        P(("fsdp", "seq"), None),
        P(("fsdp", "seq"), None),
        P(("fsdp", "seq"), None),
        P(("fsdp", "seq"), None),
        P(("fsdp", "seq")),
        P(("fsdp", "seq"), None),
        P("fsdp", "seq", None),
        P("fsdp", "seq", None),
        P("fsdp", None, "seq"),
    )
    return jax.shard_map(
        on_device,
        mesh=mesh,
        in_specs=placed,
        out_specs=(
            P("fsdp", "seq", None),
            P("fsdp", "seq", None),
            P(("fsdp", "seq")),
            P(("fsdp", "seq"), None),
            P(("fsdp", "seq"), None),
            P(("fsdp", "seq"), None),
            P(("fsdp", "seq"), None),
            P(("fsdp", "seq")),
            P(("fsdp", "seq"), None),
            P("fsdp", "seq", None),
            P("fsdp", "seq", None),
            P("fsdp", None, "seq"),
        ),
        check_vma=False,
    )
```

```python
import jax
import jax.numpy as jnp
from jax import lax
from jax.sharding import PartitionSpec as P

HD = 64


EPS = 1e-06
ATTN_MULT = 0.015625
RESID_MULT = 0.22
THETA = 10000.0
NEG_FILL = -1e30


def rope_tables(positions, head_dim):
    half_dim = head_dim // 2
    frequency = THETA ** (-(jnp.arange(half_dim, dtype=jnp.float32) * 2.0 / head_dim))
    phases = positions.astype(jnp.float32)[:, None] * frequency[None, :]
    return (jnp.cos(phases), jnp.sin(phases))


def rotate(values, cosine, sine_tab):
    half_dim = values.shape[-1] // 2
    first_half = values[..., :half_dim]
    second_half = values[..., half_dim:]
    cos_b = cosine[:, None, :]
    sin_b = sine_tab[:, None, :]
    return jnp.concatenate(
        [first_half * cos_b - second_half * sin_b, second_half * cos_b + first_half * sin_b],
        axis=-1,
    )


def unrotate(grad_vals, cosine, sine_tab):
    half_dim = grad_vals.shape[-1] // 2
    first_half = grad_vals[..., :half_dim]
    second_half = grad_vals[..., half_dim:]
    cos_b = cosine[:, None, :]
    sin_b = sine_tab[:, None, :]
    return jnp.concatenate(
        [first_half * cos_b + second_half * sin_b, second_half * cos_b - first_half * sin_b],
        axis=-1,
    )


def rms_scale(values):
    return lax.rsqrt(jnp.mean(values * values, axis=-1, keepdims=True) + EPS)


def norm_backward(inputs, scale, gain, d_normed):
    upstream = gain * d_normed
    d_inputs = scale * upstream - inputs * scale**3 * jnp.mean(
        upstream * inputs, axis=-1, keepdims=True
    )
    d_gain = jnp.sum(d_normed * inputs * scale, axis=0)
    return (d_inputs, d_gain)


def on_device(
    hidden_in,
    cotangent,
    doc_ids,
    routes,
    gain_attn,
    w_query,
    w_key,
    w_value,
    w_out,
    gain_ffn,
    w_router,
    w_gate,
    w_up,
    w_down,
):
    n_seq = lax.axis_size("seq")
    n_fsdp = lax.axis_size("fsdp")
    tok_rows = hidden_in.shape[1]
    width = hidden_in.shape[2]
    seq_len = tok_rows * n_seq
    top_k = routes.shape[2]
    n_expert = w_router.shape[1]
    local_exp = w_gate.shape[0]
    head_dim = HD
    q_width = w_query.shape[1]
    kv_width = w_key.shape[1]
    heads_here = q_width // head_dim // n_seq
    kv_here = kv_width // head_dim // n_seq
    group_size = heads_here // kv_here
    slot_cap = 3 * tok_rows * top_k // (2 * n_expert)
    f32, bf16 = jnp.float32, jnp.bfloat16
    row_own = w_query.shape[0]
    model = row_own * n_fsdp * n_seq

    def column(gain):
        return jnp.pad(gain[:, None], ((0, 0), (0, 127)))

    packed = jnp.concatenate(
        [
            w_query,
            w_key,
            w_value,
            column(gain_attn),
            w_out,
            jnp.pad(w_router, ((0, 0), (0, 128 - n_expert % 128))),
            column(gain_ffn),
        ],
        axis=1,
    )
    full = lax.all_gather(packed, ("fsdp", "seq"), axis=0, tiled=True)
    qkv_width = q_width + 2 * kv_width
    out_at = qkv_width + 128
    router_at = out_at + w_out.shape[1]
    gain_at = packed.shape[1] - 128
    full_qkv = full[:, :qkv_width]
    gain_one = full[:, qkv_width].astype(f32)
    full_out = full[:, out_at:router_at]
    full_router = full[:, router_at : router_at + n_expert]
    gain_two = full[:, gain_at].astype(f32)
    gathered_gate, gathered_up, gathered_down = (
        lax.all_gather(w_gate, "seq", axis=1, tiled=True),
        lax.all_gather(w_up, "seq", axis=1, tiled=True),
        lax.all_gather(w_down, "seq", axis=2, tiled=True),
    )

    def to_all(block):
        return lax.all_to_all(
            jnp.broadcast_to(block[None], (n_fsdp,) + block.shape),
            "fsdp",
            split_axis=0,
            concat_axis=0,
            tiled=True,
        )

    grad_in = cotangent[0]
    d_moe_all = to_all((RESID_MULT * grad_in).astype(bf16))
    routes_all = to_all(routes[0].T)
    hidden_own, d_moe_all, routes_all = lax.optimization_barrier(
        (hidden_in[0], d_moe_all, routes_all)
    )
    tokens = hidden_own.astype(f32)
    scale_one = rms_scale(tokens)
    normed_one = (tokens * scale_one * gain_one).astype(bf16)
    tok_pos = lax.axis_index("seq") * tok_rows + jnp.arange(tok_rows, dtype=jnp.int32)
    cos_tok, sin_tok = rope_tables(tok_pos, head_dim)
    qkv = jnp.dot(normed_one, full_qkv, preferred_element_type=f32)
    query = qkv[:, :q_width].reshape(tok_rows, -1, head_dim)
    keys_tok = qkv[:, q_width : q_width + kv_width].reshape(tok_rows, -1, head_dim)
    query = (
        rotate(query, cos_tok, sin_tok).astype(bf16).reshape(tok_rows, n_seq, heads_here * head_dim)
    )
    keys_tok = (
        rotate(keys_tok, cos_tok, sin_tok).astype(bf16).reshape(tok_rows, n_seq, kv_here * head_dim)
    )
    values_tok = qkv[:, q_width + kv_width :].astype(bf16)
    key_value = jnp.concatenate(
        [query, keys_tok, values_tok.reshape(tok_rows, n_seq, kv_here * head_dim)], axis=-1
    )
    recv = lax.all_to_all(key_value, "seq", split_axis=1, concat_axis=0, tiled=True)[:, 0]
    q_here = heads_here * head_dim
    k_end = q_here + kv_here * head_dim
    q_heads = recv[:, :q_here].reshape(seq_len, kv_here, group_size, head_dim)
    k_heads = recv[:, q_here:k_end].reshape(seq_len, kv_here, head_dim)
    v_heads = recv[:, k_end:].reshape(seq_len, kv_here, head_dim)
    doc_row = doc_ids[0]
    key_pos = jnp.arange(seq_len, dtype=jnp.int32)
    block_rows = min(512, seq_len)
    starts = list(range(0, seq_len, block_rows))

    def block_scores(row_start):
        row_end = row_start + block_rows
        q_blk = q_heads[row_start:row_end]
        query_pos = row_start + jnp.arange(block_rows, dtype=jnp.int32)
        allowed = (query_pos[:, None] >= key_pos[None, :row_end]) & (
            doc_row[row_start:row_end][:, None] == doc_row[None, :row_end]
        )
        scores = (
            jnp.einsum("qkgd,skd->kgqs", q_blk, k_heads[:row_end], preferred_element_type=f32)
            * ATTN_MULT
        )
        return (q_blk, jnp.where(allowed[None, None], scores, NEG_FILL))

    attn_parts = []
    lse_parts = []
    for row_start in starts:
        q_blk, scores = block_scores(row_start)
        top_val = jnp.max(scores, axis=-1, keepdims=True)
        expo_vals = jnp.exp(scores - top_val)
        row_total = jnp.sum(expo_vals, axis=-1, keepdims=True)
        lse_parts.append(top_val[..., 0] + jnp.log(row_total[..., 0]))
        prob_vals = (expo_vals / row_total).astype(bf16)
        attn_parts.append(
            jnp.einsum(
                "kgqs,skd->qkgd",
                prob_vals,
                v_heads[: row_start + block_rows],
                preferred_element_type=f32,
            ).astype(bf16)
        )
    attn_heads = jnp.concatenate(attn_parts, axis=0)
    attn_tok = lax.all_to_all(
        attn_heads.reshape(seq_len, 1, q_here),
        "seq",
        split_axis=0,
        concat_axis=1,
        tiled=True,
    ).reshape(tok_rows, q_width)
    branch = jnp.dot(attn_tok, full_out, preferred_element_type=f32)
    resid = tokens + RESID_MULT * branch
    scale_two = rms_scale(resid)
    normed_two = (resid * scale_two * gain_two).astype(bf16)
    tok_all = to_all(normed_two)

    def dense_gates(logits, route_kt):
        experts = jnp.arange(n_expert, dtype=jnp.int32)
        picked = jnp.any(route_kt[..., None] == experts, axis=-3)
        top_val = jnp.max(jnp.where(picked, logits, NEG_FILL), axis=-1, keepdims=True)
        expo_vals = jnp.where(picked, jnp.exp(jnp.where(picked, logits - top_val, 0.0)), 0.0)
        return picked, expo_vals / jnp.sum(expo_vals, axis=-1, keepdims=True)

    logits_own = jnp.dot(normed_two, full_router, preferred_element_type=f32)
    _, gates = dense_gates(logits_own, routes[0].T)
    first = lax.axis_index("fsdp") * local_exp
    picked_all, gates_all = dense_gates(
        jnp.einsum("std,de->ste", tok_all, full_router, preferred_element_type=f32), routes_all
    )
    own_picked = jnp.transpose(
        lax.dynamic_slice_in_dim(picked_all, first, local_exp, axis=2), (0, 2, 1)
    )
    own_gates = jnp.transpose(
        lax.dynamic_slice_in_dim(gates_all, first, local_exp, axis=2), (0, 2, 1)
    )
    earlier = (
        jnp.arange(tok_rows, dtype=jnp.int32)[:, None]
        < jnp.arange(tok_rows, dtype=jnp.int32)[None, :]
    ).astype(bf16)
    place = jnp.einsum(
        "seu,ut->set", own_picked.astype(bf16), earlier, preferred_element_type=f32
    ).astype(jnp.int32)
    place = jnp.where(own_picked, place, -1)
    slot_hit = place[:, :, None, :] == jnp.arange(slot_cap, dtype=jnp.int32)[:, None]
    slot_map = slot_hit.astype(bf16)
    slot_gate = jnp.sum(jnp.where(slot_hit, own_gates[:, :, None, :], 0.0), axis=-1)
    slot_gate = jnp.transpose(slot_gate, (1, 0, 2)).reshape(local_exp, n_fsdp * slot_cap, 1)
    slot_flat = slot_map.reshape(n_fsdp, local_exp * slot_cap, tok_rows)

    def to_slots(rows):
        found = jnp.einsum("sjt,std->sjd", slot_flat, rows, preferred_element_type=f32)
        found = found.astype(bf16).reshape(n_fsdp, local_exp, slot_cap, width)
        return jnp.transpose(found, (1, 0, 2, 3)).reshape(local_exp, n_fsdp * slot_cap, width)

    def from_slots(rows):
        rows = rows.reshape(local_exp, n_fsdp, slot_cap, width)
        rows = jnp.transpose(rows, (1, 0, 2, 3)).reshape(n_fsdp, local_exp * slot_cap, width)
        part = jnp.einsum("sjt,sjd->std", slot_flat, rows, preferred_element_type=f32)
        return lax.all_to_all(part.astype(bf16), "fsdp", split_axis=0, concat_axis=0, tiled=True)

    d_rows = to_slots(d_moe_all)
    inbound = to_slots(tok_all)
    pre_gate = jnp.einsum("ead,edf->eaf", inbound, gathered_gate, preferred_element_type=f32)
    pre_up = jnp.einsum("ead,edf->eaf", inbound, gathered_up, preferred_element_type=f32)
    sigm = jax.nn.sigmoid(pre_gate)
    act = pre_gate * sigm * pre_up
    act_gated = (act * slot_gate).astype(bf16)
    d_plain = jnp.einsum("ead,efd->eaf", d_rows, gathered_down, preferred_element_type=f32)
    slot_d_gate = jnp.sum(act * d_plain, axis=-1)
    d_act = d_plain * slot_gate
    d_up = (d_act * pre_gate * sigm).astype(bf16)
    d_pre_gate = (d_act * pre_up * sigm * (1.0 + pre_gate * (1.0 - sigm))).astype(bf16)
    slot_d_gate = jnp.transpose(
        slot_d_gate.reshape(local_exp, n_fsdp, slot_cap), (1, 0, 2)
    )
    d_gates_part = jnp.sum(jnp.where(slot_hit, slot_d_gate[..., None], 0.0), axis=2)
    d_gates = lax.all_to_all(d_gates_part, "fsdp", split_axis=0, concat_axis=0, tiled=True)
    d_gates = d_gates.reshape(n_expert, tok_rows).T
    seq_at = lax.axis_index("seq")

    def send_seq(grad, axis):
        step = grad.shape[axis] // n_seq

        def part(shift):
            at = lax.rem(seq_at + shift, n_seq) * step
            return lax.dynamic_slice_in_dim(grad, at, step, axis=axis)

        moved = [
            lax.ppermute(part(shift), "seq", [(i, (i + shift) % n_seq) for i in range(n_seq)])
            for shift in range(1, n_seq)
        ]
        return [part(0)] + moved

    def add_parts(parts):
        total = parts[0].astype(f32)
        for part in parts[1:]:
            total = total + part.astype(f32)
        return total

    grad_down = jnp.einsum("ead,eaf->efd", d_rows, act_gated, preferred_element_type=f32).astype(
        bf16
    )
    grad_down, d_up, d_pre_gate = lax.optimization_barrier((grad_down, d_up, d_pre_gate))
    parts_down = send_seq(grad_down, 2)
    d_inputs = (
        jnp.einsum("eaf,edf->ead", d_pre_gate, gathered_gate, preferred_element_type=f32)
        + jnp.einsum("eaf,edf->ead", d_up, gathered_up, preferred_element_type=f32)
    ).astype(bf16)
    d_parts = from_slots(d_inputs)
    grad_gate = jnp.einsum("ead,eaf->edf", inbound, d_pre_gate, preferred_element_type=f32).astype(
        bf16
    )
    grad_up = jnp.einsum("ead,eaf->edf", inbound, d_up, preferred_element_type=f32).astype(bf16)
    d_parts, grad_gate, grad_up = lax.optimization_barrier((d_parts, grad_gate, grad_up))
    parts_gate, parts_up = send_seq(grad_gate, 1), send_seq(grad_up, 1)
    d_from_experts = jnp.sum(d_parts.astype(f32), axis=0)
    expert_out = jnp.einsum("eaf,efd->ead", act_gated, gathered_down, preferred_element_type=f32)
    moe_parts = from_slots(expert_out.astype(bf16))
    output = resid + RESID_MULT * jnp.sum(moe_parts.astype(f32), axis=0)

    def sum_all(grad):
        parts = lax.all_to_all(
            grad.astype(bf16).reshape(n_fsdp, model // n_fsdp, -1),
            "fsdp",
            split_axis=0,
            concat_axis=0,
            tiled=True,
        )
        part = jnp.sum(parts.astype(f32), axis=0).astype(bf16)
        parts = lax.all_to_all(
            part.reshape(n_seq, row_own, -1), "seq", split_axis=0, concat_axis=0, tiled=True
        )
        return jnp.sum(parts.astype(f32), axis=0)

    d_chosen = gates * (d_gates - jnp.sum(gates * d_gates, axis=-1, keepdims=True))
    d_logits = d_chosen.astype(bf16)
    d_normed_two = d_from_experts + jnp.einsum(
        "te,de->td", d_logits, full_router, preferred_element_type=f32
    )
    grad_router = jnp.einsum("td,te->de", normed_two, d_logits, preferred_element_type=f32)
    d_norm_two, grad_gain_two = norm_backward(resid, scale_two, gain_two, d_normed_two)
    d_resid = grad_in + d_norm_two
    d_branch = (RESID_MULT * d_resid).astype(bf16)
    grad_out = jnp.einsum("tq,td->qd", attn_tok, d_branch, preferred_element_type=f32)
    d_attn = jnp.einsum("td,qd->tq", d_branch, full_out, preferred_element_type=f32).astype(bf16)
    own_early = sum_all(
        jnp.concatenate(
            [grad_out, jnp.pad(grad_router, ((0, 0), (0, 127 - n_expert))), grad_gain_two[:, None]],
            axis=1,
        )
    )
    d_heads = lax.all_to_all(
        d_attn.reshape(tok_rows, n_seq, q_here),
        "seq",
        split_axis=1,
        concat_axis=0,
        tiled=True,
    ).reshape(seq_len, kv_here, group_size, head_dim)
    d_query_parts = []
    d_key_sum = jnp.zeros((seq_len, kv_here, head_dim), f32)
    d_val_sum = jnp.zeros((seq_len, kv_here, head_dim), f32)
    for step, row_start in enumerate(starts):
        row_end = row_start + block_rows
        q_blk, scores = block_scores(row_start)
        prob_vals = jnp.exp(scores - lse_parts[step][..., None])
        d_out_blk = d_heads[row_start:row_end]
        attn_blk = attn_heads[row_start:row_end]
        d_val_sum = d_val_sum.at[:row_end].add(
            jnp.einsum(
                "kgqs,qkgd->skd", prob_vals.astype(bf16), d_out_blk, preferred_element_type=f32
            )
        )
        d_prob = jnp.einsum(
            "qkgd,skd->kgqs", d_out_blk, v_heads[:row_end], preferred_element_type=f32
        )
        row_delta = jnp.transpose(
            jnp.sum(d_out_blk.astype(f32) * attn_blk.astype(f32), axis=-1), (1, 2, 0)
        )
        d_score = (prob_vals * (d_prob - row_delta[..., None]) * ATTN_MULT).astype(bf16)
        d_query_parts.append(
            jnp.einsum("kgqs,skd->qkgd", d_score, k_heads[:row_end], preferred_element_type=f32)
        )
        d_key_sum = d_key_sum.at[:row_end].add(
            jnp.einsum("kgqs,qkgd->skd", d_score, q_blk, preferred_element_type=f32)
        )
    cos_full, sin_full = rope_tables(key_pos, head_dim)
    d_query_all = jnp.concatenate(d_query_parts, axis=0).reshape(seq_len, heads_here, head_dim)
    d_query_rot = unrotate(d_query_all, cos_full, sin_full).astype(bf16).reshape(seq_len, 1, q_here)
    d_key_rot = (
        unrotate(d_key_sum, cos_full, sin_full).astype(bf16).reshape(seq_len, 1, kv_here * head_dim)
    )
    d_val_low = d_val_sum.astype(bf16).reshape(seq_len, 1, kv_here * head_dim)
    d_recv = lax.all_to_all(
        jnp.concatenate([d_query_rot, d_key_rot, d_val_low], axis=-1),
        "seq",
        split_axis=0,
        concat_axis=1,
        tiled=True,
    )
    d_qkv = jnp.concatenate(
        [
            d_recv[:, :, :q_here].reshape(tok_rows, q_width),
            d_recv[:, :, q_here:k_end].reshape(tok_rows, kv_width),
            d_recv[:, :, k_end:].reshape(tok_rows, kv_width),
        ],
        axis=1,
    )
    d_normed_one = jnp.einsum("tq,dq->td", d_qkv, full_qkv, preferred_element_type=f32)
    grad_qkv = jnp.einsum("td,tq->dq", normed_one, d_qkv, preferred_element_type=f32)
    d_norm_one, grad_gain_one = norm_backward(tokens, scale_one, gain_one, d_normed_one)
    d_input = d_resid + d_norm_one
    own_late = sum_all(
        jnp.concatenate([grad_qkv, jnp.pad(grad_gain_one[:, None], ((0, 0), (0, 127)))], axis=1)
    )
    return (
        output[None],
        d_input[None],
        own_late[:, qkv_width],
        own_late[:, :q_width],
        own_late[:, q_width : q_width + kv_width],
        own_late[:, q_width + kv_width : qkv_width],
        own_early[:, :width],
        own_early[:, width + 127],
        own_early[:, width : width + n_expert],
        add_parts(parts_gate),
        add_parts(parts_up),
        add_parts(parts_down),
    )


def solution(mesh):
    placed = (
        P("fsdp", "seq", None),
        P("fsdp", "seq", None),
        P("fsdp", None),
        P("fsdp", "seq", None),
        P(("fsdp", "seq")),
        P(("fsdp", "seq"), None),
        P(("fsdp", "seq"), None),
        P(("fsdp", "seq"), None),
        P(("fsdp", "seq"), None),
        P(("fsdp", "seq")),
        P(("fsdp", "seq"), None),
        P("fsdp", "seq", None),
        P("fsdp", "seq", None),
        P("fsdp", None, "seq"),
    )
    return jax.shard_map(
        on_device,
        mesh=mesh,
        in_specs=placed,
        out_specs=(
            P("fsdp", "seq", None),
            P("fsdp", "seq", None),
            P(("fsdp", "seq")),
            P(("fsdp", "seq"), None),
            P(("fsdp", "seq"), None),
            P(("fsdp", "seq"), None),
            P(("fsdp", "seq"), None),
            P(("fsdp", "seq")),
            P(("fsdp", "seq"), None),
            P("fsdp", "seq", None),
            P("fsdp", "seq", None),
            P("fsdp", None, "seq"),
        ),
        check_vma=False,
    )
```
